32 devices in a mesh: dp: 2 (over core), expert: 16 (over z, y, x).
Axes of the slice: x: 2, y: 2, z: 4, core: 2. Of those that a mesh axis runs over, the one named last changes fastest.
Arguments:
- residual: bfloat16 [2048, 4096], P(('dp', 'expert')), may hold values from -6 to 6
- attn_out: bfloat16 [2048, 4096], P(('dp', 'expert')), may hold values from -6 to 6
- norm_gain: float32 [4096], replicated, may hold values from 0.5 to 2
- routes: int32 [2048, 8], P(('dp', 'expert')), may hold values from 0 to 15, all different within a row; in each aligned block of 64 rows (0 to 63, 64 to 127, ...) at most 40 rows name the same one
- mixing: float32 [2048, 8], P(('dp', 'expert')), may hold values from 0.05 to 0.35
- gate_w: bfloat16 [16, 4096, 768], P('expert', None, 'dp'), may hold values from -0.09375 to 0.09375
- up_w: bfloat16 [16, 4096, 768], P('expert', None, 'dp'), may hold values from -0.09375 to 0.09375
- down_w: bfloat16 [16, 768, 4096], P('expert', 'dp'), may hold values from -0.21875 to 0.21875
Outputs:
- layer_out: bfloat16 [2048, 4096], P(('dp', 'expert'))
The draws below stay inside these ranges and needn't reach their ends.
Inputs may be any that keep to these rules, and one draw needn't show every extreme that they name: `routes`: each row names 8 different experts; within the rows of one device (aligned blocks of 64 rows) no expert is named by more than 40 rows.
All inputs are finite; a program needn't handle non-finite values.
Results may differ from the reference program's by a relative error of at most 0.0041.
Values may be sent and summed in bfloat16 or wider, within the bound.
A program may use at most 128 MiB of HBM per device.

```python
import math
import jax
import jax.numpy as jnp
import numpy as np
from jax import lax

D = 4096
TOP = 8
FF = 768
ROWS_DEV = 64
EXPERTS = 16
TOKENS = 2048
CAP = 40


def block_scale(key, dims, split, smallest, largest):
    def one(axis_at, blocks):
        draws = jax.random.uniform(jax.random.fold_in(jax.random.fold_in(key, 6), axis_at), (blocks,), jnp.float32, smallest / len(split), largest / len(split))
        return jnp.repeat(jnp.exp(draws), dims[axis_at] // blocks).reshape((-1,) + (1,) * (len(dims) - axis_at - 1))

    factor_of = one(*split[0])
    for cut in split[1:]:
        factor_of = factor_of * one(*cut)
    return factor_of


def deal_out(key, own, number, rows, count, top, reach, slope):
    order = jax.random.permutation(key, count)
    crowded, common = load_shares(count, rows * top, reach, slope, True), load_shares(count, rows * top, reach, slope, False)
    places = jnp.arange(count)

    def named(tallies, offset_by):
        used = int((tallies > 0).sum())
        fixed = max(1, used // 4)
        passed = fixed + (places - fixed + offset_by * (used - fixed)) % max(1, count - fixed)
        return jnp.zeros((count,), jnp.int32).at[order[jnp.where(places < fixed, places, passed)]].set(jnp.asarray(tallies, jnp.int32))

    tallies = jnp.where(number % 4 == 0, named(crowded, number // 4), named(common, number - number // 4 - 1))
    mixed = jax.random.permutation(jax.random.fold_in(own, 3), count)
    giver, receiver = mixed[0:count // 2 * 2:2], mixed[1:count // 2 * 2:2]
    margin = jnp.minimum(tallies[giver] - 1, reach - tallies[receiver]) // 2
    margin = jnp.where((giver == order[0]) | (receiver == order[0]) | (tallies[receiver] == 0), 0, jnp.maximum(margin, 0))
    passed = jax.random.randint(jax.random.fold_in(own, 4), (count // 2,), 0, 1 << 20) % (margin + 1)
    tallies = tallies.at[giver].add(-passed).at[receiver].add(passed)
    members = jnp.searchsorted(jnp.cumsum(tallies), jnp.arange(rows * top), side="right").astype(jnp.int32)
    listing = members.reshape(top, rows).T
    listing = listing[jax.random.permutation(jax.random.fold_in(own, 1), rows)]
    offset_by = jax.random.randint(jax.random.fold_in(own, 2), (rows, 1), 0, top)
    return jnp.take_along_axis(listing, (jnp.arange(top)[None, :] + offset_by) % top, axis=1)


def load_shares(number_of, total, reach, slope, full):
    portions = [(1 << 20) // math.isqrt(rank ** slope) + 1 for rank in range(1, number_of + 1)]
    largest = reach if full else min(reach, max(-(-total // number_of), total * portions[0] // sum(portions)))
    least = 1 if total - largest >= number_of - 1 else 0
    counts, rest = [largest] + [least] * (number_of - 1), total - largest - least * (number_of - 1)
    while rest > 0:
        free = [i for i in range(1, number_of) if counts[i] < largest] or [i for i in range(1, number_of) if counts[i] < reach]
        whole, budget = sum([portions[i] for i in free]), rest
        for i in free:
            addition = min(reach - counts[i], max(1, budget * portions[i] // whole), rest)
            counts[i] = counts[i] + addition
            rest = rest - addition
    return np.array(counts)


def gaussian(stream_key, dims, width, most, cuts=(), held_as=jnp.bfloat16):
    gain = block_scale(stream_key, dims, cuts, -0.22, 0.18) if cuts else 1.0
    entries = jax.random.normal(stream_key, dims, jnp.float32) * width * gain
    return jnp.minimum(jnp.maximum(entries, -most), most).astype(held_as)


def setup_inputs(seed: int = 0) -> dict:
    key_of = jax.random.split(jax.random.key(seed), 9)
    residual = gaussian(key_of[0], (TOKENS, D), 1.0, 6.0, ((0, 32),))
    attn_out = gaussian(key_of[1], (TOKENS, D), 1.0, 6.0, ((0, 32),))
    norm_gain = jnp.clip(jnp.exp(jax.random.uniform(key_of[2], (D,), jnp.float32, math.log(0.5), math.log(2.0))), 0.5, 2.0)
    routes_keys = jax.random.split(jax.random.fold_in(key_of[3], 1), TOKENS // ROWS_DEV)
    routes_turns = jax.random.permutation(jax.random.fold_in(key_of[3], 3), TOKENS // ROWS_DEV)
    routes = jax.vmap(lambda own, number: deal_out(jax.random.fold_in(key_of[3], 2), own, number, ROWS_DEV, EXPERTS, TOP, CAP, 2))(routes_keys, routes_turns).reshape((TOKENS, TOP))
    mixing = jnp.clip(0.05 + 0.29999999 * jax.random.uniform(key_of[4], (TOKENS, TOP), jnp.float32) ** block_scale(key_of[4], (TOKENS, TOP), ((0, 32),), -0.2, 0.2), 0.05, 0.35)
    gate_w = gaussian(key_of[5], (EXPERTS, D, FF), D ** -0.5, 0.09375, ((0, 16), (2, 2)))
    up_w = gaussian(key_of[6], (EXPERTS, D, FF), D ** -0.5, 0.09375, ((0, 16), (2, 2)))
    down_w = gaussian(key_of[7], (EXPERTS, FF, D), FF ** -0.5, 0.21875, ((0, 16), (1, 2)))
    return {"residual": residual, "attn_out": attn_out, "norm_gain": norm_gain, "routes": routes, "mixing": mixing, "gate_w": gate_w, "up_w": up_w, "down_w": down_w}


def reference(residual, attn_out, norm_gain, routes, mixing, gate_w, up_w, down_w):
    stream = residual.astype(jnp.float32) + attn_out.astype(jnp.float32)
    square = lax.optimization_barrier(jnp.mean(stream * stream, axis=1, keepdims=True))
    normed = (stream * lax.rsqrt(square + 1e-06) * norm_gain[None, :]).astype(jnp.bfloat16)
    limit = TOKENS // ROWS_DEV * CAP

    def one_expert(total, which):
        hit = routes == which
        chosen = jnp.any(hit, axis=1)
        weight = lax.optimization_barrier(jnp.sum(jnp.where(hit, mixing, 0.0), axis=1))
        index = jnp.nonzero(chosen, size=limit, fill_value=0)[0]
        valid = (jnp.arange(limit) < jnp.sum(chosen.astype(jnp.int32))).astype(weight.dtype)
        picked = normed[index]
        gate = jnp.dot(picked, gate_w[which], preferred_element_type=jnp.float32)
        up = jnp.dot(picked, up_w[which], preferred_element_type=jnp.float32)
        hidden = (jax.nn.silu(gate) * up).astype(jnp.bfloat16)
        result = jnp.dot(hidden, down_w[which], preferred_element_type=jnp.float32).astype(jnp.bfloat16)
        share = result.astype(total.dtype) * (weight[index] * valid)[:, None]
        return (total.at[index].add(share), None)
    start = jnp.zeros(stream.shape, jnp.float32)
    total, _ = lax.scan(one_expert, start, jnp.arange(EXPERTS, dtype=jnp.int32))
    return (stream + total).astype(jnp.bfloat16)
```

```python
import jax
import jax.numpy as jnp
from jax import lax
from jax.sharding import PartitionSpec as P


def run_expert(inputs, gate_part, up_part, down_part):
    width = inputs.shape[-1]
    flat_rows = inputs.reshape(-1, width)
    gate = jnp.dot(flat_rows, gate_part, preferred_element_type=jnp.float32)
    up = jnp.dot(flat_rows, up_part, preferred_element_type=jnp.float32)
    hidden = (jax.nn.silu(gate) * up).astype(jnp.bfloat16)
    result = jnp.dot(hidden, down_part, preferred_element_type=jnp.float32)
    return result.reshape(inputs.shape)


def normalise(residual, attn_out, norm_gain):
    stream = residual.astype(jnp.float32) + attn_out.astype(jnp.float32)
    square = jnp.mean(stream * stream, axis=1, keepdims=True)
    normed = (stream * lax.rsqrt(square + 1e-06) * norm_gain[None, :]).astype(jnp.bfloat16)
    return stream, normed


def sparse_shards(residual, attn_out, norm_gain, routes, mixing, gate_w, up_w, down_w):
    experts = lax.axis_size("expert")
    rows, top = routes.shape
    width = residual.shape[1]
    capacity = max(2, 5 * rows * top // (4 * experts))
    slots = experts * capacity
    stream, normed = normalise(residual, attn_out, norm_gain)
    flat_routes = routes.reshape(-1)
    onehot = (flat_routes[:, None] == jnp.arange(experts, dtype=jnp.int32)[None, :]).astype(
        jnp.int32
    )
    earlier = jnp.cumsum(onehot, axis=0) - onehot
    position = jnp.sum(earlier * onehot, axis=1)
    slot_of = flat_routes * capacity + position
    selector = slot_of[None, :] == jnp.arange(slots, dtype=jnp.int32)[:, None]
    selector = jnp.any(selector.reshape(slots, rows, top), axis=2).astype(jnp.bfloat16)
    packed = jnp.dot(selector, normed, preferred_element_type=jnp.float32).astype(jnp.bfloat16)
    packed = packed.reshape(experts, capacity, width)
    gate_full, up_full = (
        lax.all_gather(gate_w, "dp", axis=2, tiled=True),
        lax.all_gather(up_w, "dp", axis=2, tiled=True),
    )
    down_full = lax.all_gather(down_w, "dp", axis=1, tiled=True)
    returned = lax.all_to_all(
        run_expert(
            lax.all_to_all(packed, "expert", split_axis=0, concat_axis=0, tiled=True),
            gate_full[0],
            up_full[0],
            down_full[0],
        ).astype(jnp.bfloat16),
        "expert",
        split_axis=0,
        concat_axis=0,
        tiled=True,
    )
    returned = returned.reshape(slots, width)
    taken = returned[slot_of].reshape(rows, top, width)
    mixed = jnp.sum(taken.astype(jnp.float32) * mixing[:, :, None], axis=1)
    return (stream + mixed).astype(jnp.bfloat16)


def dense_shards(residual, attn_out, norm_gain, routes, mixing, gate_w, up_w, down_w):
    experts = lax.axis_size("expert")
    me = lax.axis_index("expert")
    stream, normed = normalise(residual, attn_out, norm_gain)
    hit = routes[:, :, None] == jnp.arange(experts, dtype=jnp.int32)[None, None, :]
    share = jnp.sum(jnp.where(hit, mixing[:, :, None], 0.0), axis=1)
    shares = lax.all_gather(share, "expert", axis=0, tiled=True)
    tokens = lax.all_gather(normed, "expert", axis=0, tiled=True)
    gate_full = lax.all_gather(gate_w, "dp", axis=2, tiled=True)[0]
    up_full = lax.all_gather(up_w, "dp", axis=2, tiled=True)[0]
    down_full = lax.all_gather(down_w, "dp", axis=1, tiled=True)[0]
    own = jnp.sum(
        jnp.where(jnp.arange(experts)[None, :] == me, shares, 0.0), axis=1, keepdims=True
    )
    gate = jnp.dot(tokens, gate_full, preferred_element_type=jnp.float32)
    up = jnp.dot(tokens, up_full, preferred_element_type=jnp.float32)
    hidden = (jax.nn.silu(gate) * up * own).astype(jnp.bfloat16)
    result = jnp.dot(hidden, down_full, preferred_element_type=jnp.float32)
    mixed = lax.psum_scatter(
        result.astype(jnp.bfloat16), "expert", scatter_dimension=0, tiled=True
    )
    return (stream + mixed.astype(jnp.float32)).astype(jnp.bfloat16)


def shards(residual, attn_out, norm_gain, routes, *rest):
    experts = lax.axis_size("expert")
    plan = dense_shards if 2 * routes.shape[1] >= experts else sparse_shards
    return plan(residual, attn_out, norm_gain, routes, *rest)


def solution(mesh):
    return jax.shard_map(
        shards,
        mesh=mesh,
        in_specs=(
            P(("dp", "expert"), None),
            P(("dp", "expert"), None),
            P(),
            P(("dp", "expert"), None),
            P(("dp", "expert"), None),
            P("expert", None, "dp"),
            P("expert", None, "dp"),
            P("expert", "dp", None),
        ),
        out_specs=P(("dp", "expert"), None),
        check_vma=False,
    )
```

```python
import functools

import jax
import jax.numpy as jnp
from jax import lax
from jax.experimental import pallas as pl
from jax.experimental.pallas import tpu as pltpu
from jax.sharding import PartitionSpec as P


def run_expert(inputs, gate_part, up_part, down_part):
    width = inputs.shape[-1]
    flat_rows = inputs.reshape(-1, width)
    gate = jnp.dot(flat_rows, gate_part, preferred_element_type=jnp.float32)
    up = jnp.dot(flat_rows, up_part, preferred_element_type=jnp.float32)
    hidden = (jax.nn.silu(gate) * up).astype(jnp.bfloat16)
    result = jnp.dot(hidden, down_part, preferred_element_type=jnp.float32)
    return result.reshape(inputs.shape)


def normalise(residual, attn_out, norm_gain):
    stream = residual.astype(jnp.float32) + attn_out.astype(jnp.float32)
    square = jnp.mean(stream * stream, axis=1, keepdims=True)
    normed = (stream * lax.rsqrt(square + 1e-06) * norm_gain[None, :]).astype(jnp.bfloat16)
    return stream, normed


def sparse_shards(residual, attn_out, norm_gain, routes, mixing, gate_w, up_w, down_w):
    experts = lax.axis_size("expert")
    rows, top = routes.shape
    width = residual.shape[1]
    capacity = max(2, 5 * rows * top // (4 * experts))
    slots = experts * capacity
    stream, normed = normalise(residual, attn_out, norm_gain)
    flat_routes = routes.reshape(-1)
    onehot = (flat_routes[:, None] == jnp.arange(experts, dtype=jnp.int32)[None, :]).astype(
        jnp.int32
    )
    earlier = jnp.cumsum(onehot, axis=0) - onehot
    position = jnp.sum(earlier * onehot, axis=1)
    slot_of = flat_routes * capacity + position
    selector = slot_of[None, :] == jnp.arange(slots, dtype=jnp.int32)[:, None]
    selector = jnp.any(selector.reshape(slots, rows, top), axis=2).astype(jnp.bfloat16)
    packed = jnp.dot(selector, normed, preferred_element_type=jnp.float32).astype(jnp.bfloat16)
    packed = packed.reshape(experts, capacity, width)
    gate_full, up_full = (
        lax.all_gather(gate_w, "dp", axis=2, tiled=True),
        lax.all_gather(up_w, "dp", axis=2, tiled=True),
    )
    down_full = lax.all_gather(down_w, "dp", axis=1, tiled=True)
    returned = lax.all_to_all(
        run_expert(
            lax.all_to_all(packed, "expert", split_axis=0, concat_axis=0, tiled=True),
            gate_full[0],
            up_full[0],
            down_full[0],
        ).astype(jnp.bfloat16),
        "expert",
        split_axis=0,
        concat_axis=0,
        tiled=True,
    )
    returned = returned.reshape(slots, width)
    taken = returned[slot_of].reshape(rows, top, width)
    mixed = jnp.sum(taken.astype(jnp.float32) * mixing[:, :, None], axis=1)
    return (stream + mixed).astype(jnp.bfloat16)


CHUNKS = 2
MESH = pl.DeviceIdType.MESH


def fused_kernel(
    experts, x_ref, res_ref, att_ref, gate_ref, up_ref, down_ref, o_ref,
    tok, part, wg, wu, wd, hid, rb, ra, rz, fin, wsem, gsend, grecv, ssend, srecv,
):
    rows, width = o_ref.shape
    full = x_ref.shape[1]
    take = rows // CHUNKS
    chain = experts // 4
    half = width // 2
    mine = gate_ref.shape[1]
    hidden = wg.shape[1]
    htile = 256 if hidden % 256 == 0 else 128
    wtile = 512 if half % 512 == 0 else 128
    dp, me = lax.axis_index("dp"), lax.axis_index("expert")
    z, y, x = me // 4, (me // 2) % 2, me % 2
    more, less = z + 1 < chain, z > 0
    coords = ((y, x, 2, 1), (x, y, 1, 2))

    def slot(p, zz, aa, bb):
        return zz * 4 + aa * coords[p][2] + bb * coords[p][3]

    def span(j):
        return pl.ds(pl.multiple_of(j * take, take), take)

    gcols = (pl.ds(0, half), pl.ds(half, full - half))
    scols = (pl.ds(0, half), pl.ds(half, half))

    barrier = pltpu.get_barrier_semaphore()
    pl.semaphore_signal(barrier, inc=1, device_id={"dp": 1 - dp}, device_id_type=MESH)
    for p in range(2):
        a, b = coords[p][0], coords[p][1]
        pl.semaphore_signal(
            barrier, inc=1, device_id={"expert": slot(p, z, a, 1 - b)}, device_id_type=MESH
        )

    @pl.when(more)
    def _():
        pl.semaphore_signal(barrier, inc=1, device_id={"expert": me + 4}, device_id_type=MESH)

    @pl.when(less)
    def _():
        pl.semaphore_signal(barrier, inc=1, device_id={"expert": me - 4}, device_id_type=MESH)

    pl.semaphore_wait(barrier, 3 + jnp.where(more, 1, 0) + jnp.where(less, 1, 0))

    pending = []
    used = {"g": 0, "s": 0}

    def send(kind, src, dst, recv, target, cond=None):
        sems = gsend if kind == "g" else ssend
        n = used[kind]
        used[kind] = n + 1

        def copy():
            return pltpu.make_async_remote_copy(
                src_ref=src, dst_ref=dst, send_sem=sems.at[n], recv_sem=recv,
                device_id=target, device_id_type=MESH,
            )

        def go():
            copy().start()

        def end():
            copy().wait_send()

        if cond is None:
            go()
        else:
            pl.when(cond)(go)
        pending.append((cond, end))

    def arrived(dst, recv):
        pltpu.make_async_remote_copy(
            src_ref=dst, dst_ref=dst, send_sem=wsem.at[0], recv_sem=recv,
            device_id={"dp": 1 - dp}, device_id_type=MESH,
        ).wait_recv()

    columns = pl.ds(pl.multiple_of(dp * mine, 128), mine)
    lines = pl.ds(pl.multiple_of(dp * mine, 128), mine)
    others = pl.ds(pl.multiple_of((1 - dp) * mine, 128), mine)
    pairs = (
        (gate_ref, wg.at[:, columns], wg.at[:, others]),
        (up_ref, wu.at[:, columns], wu.at[:, others]),
        (down_ref, wd.at[lines, :], wd.at[others, :]),
    )

    def local(i):
        return pltpu.make_async_copy(pairs[i][0], pairs[i][1], wsem.at[1 + i])

    def remote(i):
        return pltpu.make_async_remote_copy(
            src_ref=pairs[i][0], dst_ref=pairs[i][1], send_sem=wsem.at[4 + i],
            recv_sem=wsem.at[7 + i], device_id={"dp": 1 - dp}, device_id_type=MESH,
        )

    def start_weights():
        for i in range(3):
            remote(i).start()
            local(i).start()

    def wait_weights(i):
        local(i).wait()
        arrived(pairs[i][2], wsem.at[7 + i])
        remote(i).wait_send()

    def gather_send(c, p, src, j, target, cond=None):
        send("g", src, tok.at[c, span(j), gcols[p]], grecv.at[c, p, j], {"expert": target}, cond)

    def gather_start(c, p):
        a, b = coords[p][0], coords[p][1]
        src = x_ref.at[pl.ds(c * take, take), gcols[p]]
        gather_send(c, p, src, me, slot(p, z, 1 - a, b))
        gather_send(c, p, src, me, me + 4, more)
        gather_send(c, p, src, me, me - 4, less)
        gather_send(c, p, src, me, slot(p, z, a, 1 - b))

    def gather_wait(c, p, j):
        arrived(tok.at[c, span(j), gcols[p]], grecv.at[c, p, j])

    def gather_side(c, p, zz, onward, target, cond):
        a, b = coords[p][0], coords[p][1]
        j = slot(p, zz, a, b)
        pl.when(cond)(lambda: gather_wait(c, p, j))
        src = tok.at[c, span(j), gcols[p]]
        gather_send(c, p, src, j, slot(p, z, 1 - a, b), cond)
        gather_send(c, p, src, j, target, jnp.logical_and(cond, onward))
        gather_send(c, p, src, j, slot(p, z, a, 1 - b), cond)

    def gather_chain(c, p, s):
        gather_side(c, p, z - s, more, me + 4, z - s >= 0)
        gather_side(c, p, z + s, less, me - 4, z + s < chain)

    def gather_second(c, p, s):
        a, b = coords[p][0], coords[p][1]
        sides = ((z, None),) if s == 0 else ((z - s, z - s >= 0), (z + s, z + s < chain))
        for zz, cond in sides:
            j = slot(p, zz, 1 - a, b)
            if cond is None:
                gather_wait(c, p, j)
            else:
                pl.when(cond)(functools.partial(gather_wait, c, p, j))
            src = tok.at[c, span(j), gcols[p]]
            gather_send(c, p, src, j, slot(p, z, a, 1 - b), cond)

    def gather_last(c, p):
        a, b = coords[p][0], coords[p][1]
        for zz in range(chain):
            for aa in range(2):
                gather_wait(c, p, slot(p, zz, aa, 1 - b))

    def gather_events(c):
        def both(f, *rest):
            return lambda: [f(c, p, *rest) for p in range(2)]

        def own():
            tok[c, span(me), :] = x_ref[pl.ds(c * take, take), :]

        events = [lambda: (both(gather_start)(), own())]
        for s in range(chain):
            if s > 0:
                events.append(both(gather_chain, s))
            events.append(both(gather_second, s))
        events.append(both(gather_last))
        return events

    def shares(c):
        extra = tok[c, :, pl.ds(width, full - width)].astype(jnp.float32)
        lane = lax.broadcasted_iota(jnp.int32, extra.shape, 1)
        keep = jnp.logical_or(lane == me, lane == experts + me)
        return jnp.sum(jnp.where(keep, extra, 0.0), axis=1, keepdims=True)

    def expert_in(c, n):
        cut = pl.ds(n * htile, htile)
        values = tok[c, :, pl.ds(0, width)]
        gate = jnp.dot(values, wg[:, cut], preferred_element_type=jnp.float32)
        up = jnp.dot(values, wu[:, cut], preferred_element_type=jnp.float32)
        act = gate / (1.0 + jnp.exp(-gate)) * up * shares(c)
        hid[:, cut] = act.astype(hid.dtype)

    def expert_out(c, p):
        @pl.loop(0, half // wtile)
        def _(n):
            cut = pl.ds(pl.multiple_of(p * half + n * wtile, wtile), wtile)
            done = jnp.dot(hid[...], wd[:, cut], preferred_element_type=jnp.float32)
            part[c, :, cut] = done.astype(part.dtype)

    def expert_events(c):
        events = []
        for n in range(hidden // htile):
            events.append(functools.partial(expert_in, c, n))
        for p in range(2):
            events.append(lambda p=p: (expert_out(c, p), scatter_first(c, p)))
        return events

    def scatter_first(c, p):
        a, b = coords[p][0], coords[p][1]
        for aa in (1 - a, a):
            for zz in range(chain):
                src = part.at[c, span(slot(p, zz, aa, 1 - b)), scols[p]]
                k = zz * 2 + aa
                send("s", src, rb.at[c, p, k], srecv.at[c, p, k],
                     {"expert": slot(p, z, a, 1 - b)})

    def scatter_second(c, p, zz):
        a, b = coords[p][0], coords[p][1]
        k = zz * 2 + 1 - a
        arrived(rb.at[c, p, k], srecv.at[c, p, k])
        here = (c, span(slot(p, zz, 1 - a, b)), scols[p])
        both = part[here].astype(jnp.float32) + rb[c, p, k].astype(jnp.float32)
        part[here] = both.astype(part.dtype)
        send("s", part.at[here], ra.at[c, p, zz], srecv.at[c, p, 2 * chain + zz],
             {"expert": slot(p, z, 1 - a, b)})

    def summed(c, p, zz):
        a, b = coords[p][0], coords[p][1]
        k = zz * 2 + a
        arrived(rb.at[c, p, k], srecv.at[c, p, k])
        arrived(ra.at[c, p, zz], srecv.at[c, p, 2 * chain + zz])
        own = part[c, span(slot(p, zz, a, b)), scols[p]].astype(jnp.float32)
        return own + rb[c, p, k].astype(jnp.float32) + ra[c, p, zz].astype(jnp.float32)

    def passing(c, p, way, zz):
        k = (3 + way) * chain + zz
        arrived(rz.at[c, p, way, zz], srecv.at[c, p, k])
        return rz[c, p, way, zz].astype(jnp.float32)

    def scatter_side(c, p, way, zz, cond, behind, target):
        a, b = coords[p][0], coords[p][1]
        here = (c, span(slot(p, zz, a, b)), scols[p])

        @pl.when(cond)
        def _():
            part[here] = summed(c, p, zz).astype(part.dtype)

        @pl.when(jnp.logical_and(cond, behind))
        def _():
            more_of = part[here].astype(jnp.float32) + passing(c, p, way, zz)
            part[here] = more_of.astype(part.dtype)

        send("s", part.at[here], rz.at[c, p, way, zz],
             srecv.at[c, p, (3 + way) * chain + zz], {"expert": target}, cond)

    def scatter_chain(c, p, s):
        scatter_side(c, p, 0, z + s, z + s < chain, less, me + 4)
        scatter_side(c, p, 1, z - s, z - s >= 0, more, me - 4)

    def scatter_last(c, p):
        lines = pl.ds(c * take, take)
        total = summed(c, p, z)
        stream = res_ref[lines, scols[p]].astype(jnp.float32) + att_ref[
            lines, scols[p]
        ].astype(jnp.float32)
        fin[:, :] = total

        @pl.when(less)
        def _():
            fin[:, :] += passing(c, p, 0, z)

        @pl.when(more)
        def _():
            fin[:, :] += passing(c, p, 1, z)

        o_ref[lines, scols[p]] = (stream + fin[:, :]).astype(o_ref.dtype)

    def scatter_events(c):
        def both(f, *rest):
            return lambda: [f(c, p, *rest) for p in range(2)]

        events = [both(scatter_second, zz) for zz in range(chain)]
        events += [both(scatter_chain, s) for s in range(chain - 1, 0, -1)]
        events.append(both(scatter_last))
        return events

    def merged(first, second):
        out = []
        for i in range(max(len(first), len(second))):
            out += first[i : i + 1] + second[i : i + 1]
        return out

    fetch = [gather_events(c) for c in range(CHUNKS)]
    work = [expert_events(c) for c in range(CHUNKS)]
    back = [scatter_events(c) for c in range(CHUNKS)]
    order = fetch[0][:1] + [start_weights] + fetch[0][1:3] + fetch[1][:1] + fetch[0][3:]
    order += [lambda: [wait_weights(i) for i in range(3)]]
    order += merged(fetch[1][1:], work[0])
    order += merged(work[1], back[0]) + back[1]
    for event in order:
        event()
    for cond, end in pending:
        if cond is None:
            end()
        else:
            pl.when(cond)(end)


def multicast_shards(residual, attn_out, norm_gain, routes, mixing, gate_w, up_w, down_w):
    experts = lax.axis_size("expert")
    rows, width = residual.shape
    mine = gate_w.shape[2]
    hidden = mine * lax.axis_size("dp")
    lanes = -(-2 * experts // 128) * 128
    full = width + lanes
    take, chain = rows // CHUNKS, experts // 4
    _, normed = normalise(residual, attn_out, norm_gain)
    hit = routes[:, :, None] == jnp.arange(experts, dtype=jnp.int32)[None, None, :]
    share = jnp.sum(jnp.where(hit, mixing[:, :, None], 0.0), axis=1)
    high = lax.reduce_precision(share, 8, 7)
    extra = jnp.concatenate([high, share - high], axis=1).astype(jnp.bfloat16)
    extra = jnp.pad(extra, ((0, 0), (0, lanes - 2 * experts)))
    packed = jnp.concatenate([normed, extra], axis=1)
    bf16 = jnp.bfloat16
    copies = 2 * CHUNKS * (4 + 6 * (chain - 1) + 1 + 2 * (chain - 1))
    sums = 2 * CHUNKS * (3 * chain + 2 * (chain - 1))
    vmem, anywhere = pl.BlockSpec(memory_space=pltpu.VMEM), pl.BlockSpec(memory_space=pl.ANY)
    return pl.pallas_call(
        functools.partial(fused_kernel, experts),
        out_shape=jax.ShapeDtypeStruct((rows, width), bf16),
        in_specs=[vmem] * 3 + [anywhere] * 3,
        out_specs=vmem,
        scratch_shapes=[
            pltpu.VMEM((CHUNKS, experts * take, full), bf16),
            pltpu.VMEM((CHUNKS, experts * take, width), bf16),
            pltpu.VMEM((width, hidden), bf16),
            pltpu.VMEM((width, hidden), bf16),
            pltpu.VMEM((hidden, width), bf16),
            pltpu.VMEM((experts * take, hidden), bf16),
            pltpu.VMEM((CHUNKS, 2, 2 * chain, take, width // 2), bf16),
            pltpu.VMEM((CHUNKS, 2, chain, take, width // 2), bf16),
            pltpu.VMEM((CHUNKS, 2, 2, chain, take, width // 2), bf16),
            pltpu.VMEM((take, width // 2), jnp.float32),
            pltpu.SemaphoreType.DMA((10,)),
            pltpu.SemaphoreType.DMA((copies,)),
            pltpu.SemaphoreType.DMA((CHUNKS, 2, experts)),
            pltpu.SemaphoreType.DMA((sums,)),
            pltpu.SemaphoreType.DMA((CHUNKS, 2, 5 * chain)),
        ],
        compiler_params=pltpu.CompilerParams(
            collective_id=0, has_side_effects=True, vmem_limit_bytes=66 * 1000 * 1000
        ),
    )(packed, residual, attn_out, gate_w[0], up_w[0], down_w[0])


def shards(residual, attn_out, norm_gain, routes, *rest):
    experts = lax.axis_size("expert")
    paired = lax.axis_size("dp") == 2 and experts % 4 == 0 and residual.shape[0] % 32 == 0
    wide = 2 * routes.shape[1] >= experts
    plan = multicast_shards if paired and wide else sparse_shards
    return plan(residual, attn_out, norm_gain, routes, *rest)


def solution(mesh):
    return jax.shard_map(
        shards,
        mesh=mesh,
        in_specs=(
            P(("dp", "expert"), None),
            P(("dp", "expert"), None),
            P(),
            P(("dp", "expert"), None),
            P(("dp", "expert"), None),
            P("expert", None, "dp"),
            P("expert", None, "dp"),
            P("expert", "dp", None),
        ),
        out_specs=P(("dp", "expert"), None),
        check_vma=False,
    )
```

```python
import functools

import jax
import jax.numpy as jnp
from jax import lax
from jax.experimental import pallas as pl
from jax.experimental.pallas import tpu as pltpu
from jax.sharding import PartitionSpec as P


def run_expert(inputs, gate_part, up_part, down_part):
    width = inputs.shape[-1]
    flat_rows = inputs.reshape(-1, width)
    gate = jnp.dot(flat_rows, gate_part, preferred_element_type=jnp.float32)
    up = jnp.dot(flat_rows, up_part, preferred_element_type=jnp.float32)
    hidden = (jax.nn.silu(gate) * up).astype(jnp.bfloat16)
    result = jnp.dot(hidden, down_part, preferred_element_type=jnp.float32)
    return result.reshape(inputs.shape)


def normalise(residual, attn_out, norm_gain):
    stream = residual.astype(jnp.float32) + attn_out.astype(jnp.float32)
    square = jnp.mean(stream * stream, axis=1, keepdims=True)
    normed = (stream * lax.rsqrt(square + 1e-06) * norm_gain[None, :]).astype(jnp.bfloat16)
    return stream, normed


def sparse_shards(residual, attn_out, norm_gain, routes, mixing, gate_w, up_w, down_w):
    experts = lax.axis_size("expert")
    rows, top = routes.shape
    width = residual.shape[1]
    capacity = max(2, 5 * rows * top // (4 * experts))
    slots = experts * capacity
    stream, normed = normalise(residual, attn_out, norm_gain)
    flat_routes = routes.reshape(-1)
    onehot = (flat_routes[:, None] == jnp.arange(experts, dtype=jnp.int32)[None, :]).astype(
        jnp.int32
    )
    earlier = jnp.cumsum(onehot, axis=0) - onehot
    position = jnp.sum(earlier * onehot, axis=1)
    slot_of = flat_routes * capacity + position
    selector = slot_of[None, :] == jnp.arange(slots, dtype=jnp.int32)[:, None]
    selector = jnp.any(selector.reshape(slots, rows, top), axis=2).astype(jnp.bfloat16)
    packed = jnp.dot(selector, normed, preferred_element_type=jnp.float32).astype(jnp.bfloat16)
    packed = packed.reshape(experts, capacity, width)
    gate_full, up_full = (
        lax.all_gather(gate_w, "dp", axis=2, tiled=True),
        lax.all_gather(up_w, "dp", axis=2, tiled=True),
    )
    down_full = lax.all_gather(down_w, "dp", axis=1, tiled=True)
    returned = lax.all_to_all(
        run_expert(
            lax.all_to_all(packed, "expert", split_axis=0, concat_axis=0, tiled=True),
            gate_full[0],
            up_full[0],
            down_full[0],
        ).astype(jnp.bfloat16),
        "expert",
        split_axis=0,
        concat_axis=0,
        tiled=True,
    )
    returned = returned.reshape(slots, width)
    taken = returned[slot_of].reshape(rows, top, width)
    mixed = jnp.sum(taken.astype(jnp.float32) * mixing[:, :, None], axis=1)
    return (stream + mixed).astype(jnp.bfloat16)


CHUNKS = 2
PARTS = 4
MESH = pl.DeviceIdType.MESH


def fused_kernel(
    experts, x_ref, res_ref, att_ref, gate_ref, up_ref, down_ref, o_ref,
    tok, part, wg, wu, wd, hid, rb, ra, rz, fin, wsem, gsend, grecv, ssend, srecv,
):
    rows, width = o_ref.shape
    full = x_ref.shape[1]
    take = rows // CHUNKS
    chain = experts // 4
    piece = width // PARTS
    mine = gate_ref.shape[1]
    hidden = wg.shape[1]
    htile = 256 if hidden % 256 == 0 else 128
    wtile = 512 if piece % 512 == 0 else 128
    dp, me = lax.axis_index("dp"), lax.axis_index("expert")
    z, y, x = me // 4, (me // 2) % 2, me % 2
    more, less = z + 1 < chain, z > 0
    coords = ((x, y, 1, 2), (y, x, 2, 1), (y, x, 2, 1), (x, y, 1, 2))
    early, late = (0, 1), (2, 3)
    every = early + late

    def slot(p, zz, aa, bb):
        return zz * 4 + aa * coords[p][2] + bb * coords[p][3]

    def span(j):
        return pl.ds(pl.multiple_of(j * take, take), take)

    scols = [pl.ds(p * piece, piece) for p in every]
    gcols = scols[:-1] + [pl.ds(width - piece, full - width + piece)]

    barrier = pltpu.get_barrier_semaphore()
    pl.semaphore_signal(barrier, inc=1, device_id={"dp": 1 - dp}, device_id_type=MESH)
    for p in late:
        a, b = coords[p][0], coords[p][1]
        pl.semaphore_signal(
            barrier, inc=1, device_id={"expert": slot(p, z, a, 1 - b)}, device_id_type=MESH
        )

    @pl.when(more)
    def _():
        pl.semaphore_signal(barrier, inc=1, device_id={"expert": me + 4}, device_id_type=MESH)

    @pl.when(less)
    def _():
        pl.semaphore_signal(barrier, inc=1, device_id={"expert": me - 4}, device_id_type=MESH)

    pl.semaphore_wait(barrier, 3 + jnp.where(more, 1, 0) + jnp.where(less, 1, 0))

    pending = []
    used = {"g": 0, "s": 0}

    def send(kind, src, dst, recv, target, cond=None):
        sems = gsend if kind == "g" else ssend
        n = used[kind]
        used[kind] = n + 1

        def copy():
            return pltpu.make_async_remote_copy(
                src_ref=src, dst_ref=dst, send_sem=sems.at[n], recv_sem=recv,
                device_id=target, device_id_type=MESH,
            )

        def go():
            copy().start()

        def end():
            copy().wait_send()

        if cond is None:
            go()
        else:
            pl.when(cond)(go)
        pending.append((cond, end))

    def arrived(dst, recv):
        pltpu.make_async_remote_copy(
            src_ref=dst, dst_ref=dst, send_sem=wsem.at[0], recv_sem=recv,
            device_id={"dp": 1 - dp}, device_id_type=MESH,
        ).wait_recv()

    columns = pl.ds(pl.multiple_of(dp * mine, 128), mine)
    lines = pl.ds(pl.multiple_of(dp * mine, 128), mine)
    others = pl.ds(pl.multiple_of((1 - dp) * mine, 128), mine)
    pairs = (
        (gate_ref, wg.at[:, columns], wg.at[:, others]),
        (up_ref, wu.at[:, columns], wu.at[:, others]),
        (down_ref, wd.at[lines, :], wd.at[others, :]),
    )

    def local(i):
        return pltpu.make_async_copy(pairs[i][0], pairs[i][1], wsem.at[1 + i])

    def remote(i):
        return pltpu.make_async_remote_copy(
            src_ref=pairs[i][0], dst_ref=pairs[i][1], send_sem=wsem.at[4 + i],
            recv_sem=wsem.at[7 + i], device_id={"dp": 1 - dp}, device_id_type=MESH,
        )

    def start_weights():
        for i in range(3):
            remote(i).start()
            local(i).start()

    def wait_weights(i):
        local(i).wait()
        arrived(pairs[i][2], wsem.at[7 + i])
        remote(i).wait_send()

    def gather_send(c, p, src, j, target, cond=None):
        send("g", src, tok.at[c, span(j), gcols[p]], grecv.at[c, p, j], {"expert": target}, cond)

    def gather_start(c, p):
        a, b = coords[p][0], coords[p][1]
        src = x_ref.at[pl.ds(c * take, take), gcols[p]]
        gather_send(c, p, src, me, slot(p, z, 1 - a, b))
        gather_send(c, p, src, me, me + 4, more)
        gather_send(c, p, src, me, me - 4, less)
        gather_send(c, p, src, me, slot(p, z, a, 1 - b))

    def gather_wait(c, p, j):
        arrived(tok.at[c, span(j), gcols[p]], grecv.at[c, p, j])

    def gather_turn(c, p):
        a, b = coords[p][0], coords[p][1]
        j = slot(p, z, 1 - a, b)
        gather_wait(c, p, j)
        src = tok.at[c, span(j), gcols[p]]
        gather_send(c, p, src, j, me + 4, more)
        gather_send(c, p, src, j, me - 4, less)
        gather_send(c, p, src, j, slot(p, z, a, 1 - b))

    def gather_side(c, p, zz, aa, onward, target, cond):
        a, b = coords[p][0], coords[p][1]
        j = slot(p, zz, aa, b)
        pl.when(cond)(lambda: gather_wait(c, p, j))
        src = tok.at[c, span(j), gcols[p]]
        if p in late:
            gather_send(c, p, src, j, slot(p, z, 1 - a, b), cond)
        gather_send(c, p, src, j, target, jnp.logical_and(cond, onward))
        gather_send(c, p, src, j, slot(p, z, a, 1 - b), cond)

    def gather_chain(c, p, s):
        a = coords[p][0]
        for aa in (a, 1 - a) if p in early else (a,):
            gather_side(c, p, z - s, aa, more, me + 4, z - s >= 0)
            gather_side(c, p, z + s, aa, less, me - 4, z + s < chain)

    def gather_second(c, p, s):
        a, b = coords[p][0], coords[p][1]
        sides = ((z, None),) if s == 0 else ((z - s, z - s >= 0), (z + s, z + s < chain))
        for zz, cond in sides:
            j = slot(p, zz, 1 - a, b)
            if cond is None:
                gather_wait(c, p, j)
            else:
                pl.when(cond)(functools.partial(gather_wait, c, p, j))
            src = tok.at[c, span(j), gcols[p]]
            gather_send(c, p, src, j, slot(p, z, a, 1 - b), cond)

    def gather_last(c, p):
        a, b = coords[p][0], coords[p][1]
        for zz in range(chain):
            for aa in range(2):
                gather_wait(c, p, slot(p, zz, aa, 1 - b))

    def over(parts, f, *rest):
        return lambda: [f(rest[0], p, *rest[1:]) for p in parts]

    def gather_events(c):
        def own():
            tok[c, span(me), :] = x_ref[pl.ds(c * take, take), :]

        events = [lambda: (over(every, gather_start, c)(), own())]
        events.append(over(early, gather_turn, c))
        for s in range(1, chain):
            events.append(over(late, gather_chain, c, s))
            events.append(over(late, gather_second, c, s - 1))
            events.append(over(early, gather_chain, c, s))
        events.append(over(late, gather_second, c, chain - 1))
        events.append(over(every, gather_last, c))
        return events

    def shares(c):
        extra = tok[c, :, pl.ds(width, full - width)].astype(jnp.float32)
        lane = lax.broadcasted_iota(jnp.int32, extra.shape, 1)
        keep = jnp.logical_or(lane == me, lane == experts + me)
        return jnp.sum(jnp.where(keep, extra, 0.0), axis=1, keepdims=True)

    def expert_in(c, n):
        cut = pl.ds(n * htile, htile)
        values = tok[c, :, pl.ds(0, width)]
        gate = jnp.dot(values, wg[:, cut], preferred_element_type=jnp.float32)
        up = jnp.dot(values, wu[:, cut], preferred_element_type=jnp.float32)
        act = gate / (1.0 + jnp.exp(-gate)) * up * shares(c)
        hid[:, cut] = act.astype(hid.dtype)

    def expert_out(c, p):
        @pl.loop(0, piece // wtile)
        def _(n):
            cut = pl.ds(pl.multiple_of(p * piece + n * wtile, wtile), wtile)
            done = jnp.dot(hid[...], wd[:, cut], preferred_element_type=jnp.float32)
            part[c, :, cut] = done.astype(part.dtype)

    def expert_events(c):
        events = []
        for n in range(hidden // htile):
            events.append(functools.partial(expert_in, c, n))
        for p in every:
            events.append(lambda p=p: (expert_out(c, p), scatter_first(c, p)))
        return events

    def scatter_first(c, p):
        a, b = coords[p][0], coords[p][1]
        far = [(z + chain - 1 - i) % chain for i in range(chain)]
        dests = [(zz, aa) for aa in (1 - a, a) for zz in far]
        if p in early:
            dests = [(zz, aa) for zz in far for aa in (1 - a, a)]
        for zz, aa in dests:
            src = part.at[c, span(slot(p, zz, aa, 1 - b)), scols[p]]
            k = zz * 2 + aa
            send("s", src, rb.at[c, p, k], srecv.at[c, p, k],
                 {"expert": slot(p, z, a, 1 - b)})

    def scatter_second(c, p, i):
        a, b = coords[p][0], coords[p][1]
        zz = (z + chain - 1 - i) % chain
        k = zz * 2 + 1 - a
        arrived(rb.at[c, p, k], srecv.at[c, p, k])
        here = (c, span(slot(p, zz, 1 - a, b)), scols[p])
        both = part[here].astype(jnp.float32) + rb[c, p, k].astype(jnp.float32)
        part[here] = both.astype(part.dtype)
        send("s", part.at[here], ra.at[c, p, zz], srecv.at[c, p, 2 * chain + zz],
             {"expert": slot(p, z, 1 - a, b)})

    def summed(c, p, zz, aa):
        b = coords[p][1]
        k = zz * 2 + aa
        arrived(rb.at[c, p, k], srecv.at[c, p, k])
        own = part[c, span(slot(p, zz, aa, b)), scols[p]].astype(jnp.float32)
        total = own + rb[c, p, k].astype(jnp.float32)
        if p in late:
            arrived(ra.at[c, p, zz], srecv.at[c, p, 2 * chain + zz])
            total += ra[c, p, zz].astype(jnp.float32)
        return total

    def passing(c, p, way, zz, aa):
        k = (zz * 2 + aa) * 2 + way
        arrived(rz.at[c, p, k], srecv.at[c, p, 3 * chain + k])
        return rz[c, p, k].astype(jnp.float32)

    def scatter_side(c, p, way, zz, aa, cond, behind, target):
        here = (c, span(slot(p, zz, aa, coords[p][1])), scols[p])
        k = (zz * 2 + aa) * 2 + way

        @pl.when(jnp.logical_and(cond, jnp.logical_not(behind)))
        def _():
            part[here] = summed(c, p, zz, aa).astype(part.dtype)

        @pl.when(jnp.logical_and(cond, behind))
        def _():
            total = summed(c, p, zz, aa) + passing(c, p, way, zz, aa)
            part[here] = total.astype(part.dtype)

        send("s", part.at[here], rz.at[c, p, k], srecv.at[c, p, 3 * chain + k],
             {"expert": target}, cond)

    def scatter_chain(c, p, s):
        a = coords[p][0]
        for aa in (1 - a, a) if p in early else (a,):
            scatter_side(c, p, 0, z + s, aa, z + s < chain, less, me + 4)
            scatter_side(c, p, 1, z - s, aa, z - s >= 0, more, me - 4)

    def landed(c, p, aa):
        fin[:, :] = summed(c, p, z, aa)

        @pl.when(less)
        def _():
            fin[:, :] += passing(c, p, 0, z, aa)

        @pl.when(more)
        def _():
            fin[:, :] += passing(c, p, 1, z, aa)

    def scatter_turn(c, p):
        a, b = coords[p][0], coords[p][1]
        landed(c, p, 1 - a)
        here = (c, span(slot(p, z, 1 - a, b)), scols[p])
        part[here] = fin[:, :].astype(part.dtype)
        send("s", part.at[here], ra.at[c, p, 0], srecv.at[c, p, 2 * chain],
             {"expert": slot(p, z, 1 - a, b)})

    def scatter_last(c, p):
        lines = pl.ds(c * take, take)
        landed(c, p, coords[p][0])
        stream = res_ref[lines, scols[p]].astype(jnp.float32) + att_ref[
            lines, scols[p]
        ].astype(jnp.float32)
        total = stream + fin[:, :]
        if p in early:
            arrived(ra.at[c, p, 0], srecv.at[c, p, 2 * chain])
            total += ra[c, p, 0].astype(jnp.float32)
        o_ref[lines, scols[p]] = total.astype(o_ref.dtype)

    def scatter_events(c):
        events = []
        for s in range(chain - 1, 0, -1):
            events.append(over(early, scatter_chain, c, s))
            events.append(over(late, scatter_second, c, chain - 1 - s))
        events.append(over(late, scatter_second, c, chain - 1))
        events.append(over(early, scatter_turn, c))
        for s in range(chain - 1, 0, -1):
            events.append(over(late, scatter_chain, c, s))
        events.append(over(late, scatter_last, c))
        events.append(over(early, scatter_last, c))
        return events

    def merged(first, second):
        out = []
        for i in range(max(len(first), len(second))):
            out += first[i : i + 1] + second[i : i + 1]
        return out

    fetch = [gather_events(c) for c in range(CHUNKS)]
    work = [expert_events(c) for c in range(CHUNKS)]
    back = [scatter_events(c) for c in range(CHUNKS)]
    order = fetch[0][:1] + [start_weights] + fetch[0][1:3] + fetch[1][:1] + fetch[0][3:]
    order += [lambda: [wait_weights(i) for i in range(3)]]
    order += merged(fetch[1][1:], work[0])
    order += merged(work[1], back[0][:7]) + merged(back[0][7:], back[1][:7]) + back[1][7:]
    for event in order:
        event()
    for cond, end in pending:
        if cond is None:
            end()
        else:
            pl.when(cond)(end)


def multicast_shards(residual, attn_out, norm_gain, routes, mixing, gate_w, up_w, down_w):
    experts = lax.axis_size("expert")
    rows, width = residual.shape
    mine = gate_w.shape[2]
    hidden = mine * lax.axis_size("dp")
    lanes = -(-2 * experts // 128) * 128
    full = width + lanes
    take, chain = rows // CHUNKS, experts // 4
    _, normed = normalise(residual, attn_out, norm_gain)
    hit = routes[:, :, None] == jnp.arange(experts, dtype=jnp.int32)[None, None, :]
    share = jnp.sum(jnp.where(hit, mixing[:, :, None], 0.0), axis=1)
    high = lax.reduce_precision(share, 8, 7)
    extra = jnp.concatenate([high, share - high], axis=1).astype(jnp.bfloat16)
    extra = jnp.pad(extra, ((0, 0), (0, lanes - 2 * experts)))
    packed = jnp.concatenate([normed, extra], axis=1)
    bf16 = jnp.bfloat16
    copies = PARTS * CHUNKS * (7 + 8 * (chain - 1))
    sums = PARTS * CHUNKS * (1 + 3 * chain + 4 * (chain - 1))
    vmem, anywhere = pl.BlockSpec(memory_space=pltpu.VMEM), pl.BlockSpec(memory_space=pl.ANY)
    return pl.pallas_call(
        functools.partial(fused_kernel, experts),
        out_shape=jax.ShapeDtypeStruct((rows, width), bf16),
        in_specs=[vmem] * 3 + [anywhere] * 3,
        out_specs=vmem,
        scratch_shapes=[
            pltpu.VMEM((CHUNKS, experts * take, full), bf16),
            pltpu.VMEM((CHUNKS, experts * take, width), bf16),
            pltpu.VMEM((width, hidden), bf16),
            pltpu.VMEM((width, hidden), bf16),
            pltpu.VMEM((hidden, width), bf16),
            pltpu.VMEM((experts * take, hidden), bf16),
            pltpu.VMEM((CHUNKS, PARTS, 2 * chain, take, width // PARTS), bf16),
            pltpu.VMEM((CHUNKS, PARTS, chain, take, width // PARTS), bf16),
            pltpu.VMEM((CHUNKS, PARTS, 4 * chain, take, width // PARTS), bf16),
            pltpu.VMEM((take, width // PARTS), jnp.float32),
            pltpu.SemaphoreType.DMA((10,)),
            pltpu.SemaphoreType.DMA((copies,)),
            pltpu.SemaphoreType.DMA((CHUNKS, PARTS, experts)),
            pltpu.SemaphoreType.DMA((sums,)),
            pltpu.SemaphoreType.DMA((CHUNKS, PARTS, 7 * chain)),
        ],
        compiler_params=pltpu.CompilerParams(
            collective_id=0, has_side_effects=True, vmem_limit_bytes=66 * 1000 * 1000
        ),
    )(packed, residual, attn_out, gate_w[0], up_w[0], down_w[0])


def shards(residual, attn_out, norm_gain, routes, *rest):
    experts = lax.axis_size("expert")
    paired = lax.axis_size("dp") == 2 and experts % 4 == 0 and residual.shape[0] % 32 == 0
    wide = 2 * routes.shape[1] >= experts
    plan = multicast_shards if paired and wide else sparse_shards
    return plan(residual, attn_out, norm_gain, routes, *rest)


def solution(mesh):
    return jax.shard_map(
        shards,
        mesh=mesh,
        in_specs=(
            P(("dp", "expert"), None),
            P(("dp", "expert"), None),
            P(),
            P(("dp", "expert"), None),
            P(("dp", "expert"), None),
            P("expert", None, "dp"),
            P("expert", None, "dp"),
            P("expert", "dp", None),
        ),
        out_specs=P(("dp", "expert"), None),
        check_vma=False,
    )
```

```python
import functools

import jax
import jax.numpy as jnp
from jax import lax
from jax.experimental import pallas as pl
from jax.experimental.pallas import tpu as pltpu
from jax.sharding import PartitionSpec as P


def run_expert(inputs, gate_part, up_part, down_part):
    width = inputs.shape[-1]
    flat_rows = inputs.reshape(-1, width)
    gate = jnp.dot(flat_rows, gate_part, preferred_element_type=jnp.float32)
    up = jnp.dot(flat_rows, up_part, preferred_element_type=jnp.float32)
    hidden = (jax.nn.silu(gate) * up).astype(jnp.bfloat16)
    result = jnp.dot(hidden, down_part, preferred_element_type=jnp.float32)
    return result.reshape(inputs.shape)


def normalise(residual, attn_out, norm_gain):
    stream = residual.astype(jnp.float32) + attn_out.astype(jnp.float32)
    square = jnp.mean(stream * stream, axis=1, keepdims=True)
    normed = (stream * lax.rsqrt(square + 1e-06) * norm_gain[None, :]).astype(jnp.bfloat16)
    return stream, normed


def sparse_shards(residual, attn_out, norm_gain, routes, mixing, gate_w, up_w, down_w):
    experts = lax.axis_size("expert")
    rows, top = routes.shape
    width = residual.shape[1]
    capacity = max(2, 5 * rows * top // (4 * experts))
    slots = experts * capacity
    stream, normed = normalise(residual, attn_out, norm_gain)
    flat_routes = routes.reshape(-1)
    onehot = (flat_routes[:, None] == jnp.arange(experts, dtype=jnp.int32)[None, :]).astype(
        jnp.int32
    )
    earlier = jnp.cumsum(onehot, axis=0) - onehot
    position = jnp.sum(earlier * onehot, axis=1)
    slot_of = flat_routes * capacity + position
    selector = slot_of[None, :] == jnp.arange(slots, dtype=jnp.int32)[:, None]
    selector = jnp.any(selector.reshape(slots, rows, top), axis=2).astype(jnp.bfloat16)
    packed = jnp.dot(selector, normed, preferred_element_type=jnp.float32).astype(jnp.bfloat16)
    packed = packed.reshape(experts, capacity, width)
    gate_full, up_full = (
        lax.all_gather(gate_w, "dp", axis=2, tiled=True),
        lax.all_gather(up_w, "dp", axis=2, tiled=True),
    )
    down_full = lax.all_gather(down_w, "dp", axis=1, tiled=True)
    returned = lax.all_to_all(
        run_expert(
            lax.all_to_all(packed, "expert", split_axis=0, concat_axis=0, tiled=True),
            gate_full[0],
            up_full[0],
            down_full[0],
        ).astype(jnp.bfloat16),
        "expert",
        split_axis=0,
        concat_axis=0,
        tiled=True,
    )
    returned = returned.reshape(slots, width)
    taken = returned[slot_of].reshape(rows, top, width)
    mixed = jnp.sum(taken.astype(jnp.float32) * mixing[:, :, None], axis=1)
    return (stream + mixed).astype(jnp.bfloat16)


CHUNKS = 2
PARTS = 4
MESH = pl.DeviceIdType.MESH


def fused_kernel(
    experts, x_ref, res_ref, att_ref, gate_ref, up_ref, down_ref, o_ref,
    tok, part, wg, wu, wd, hid, rb, ra, rz, fin, wsem, gsend, grecv, ssend, srecv,
):
    rows, width = o_ref.shape
    full = x_ref.shape[1]
    take = rows // CHUNKS
    chain = experts // 4
    piece = width // PARTS
    mine = gate_ref.shape[1]
    hidden = wg.shape[1]
    htile = 256 if hidden % 256 == 0 else 128
    wtile = 512 if piece % 512 == 0 else 128
    dp, me = lax.axis_index("dp"), lax.axis_index("expert")
    z, y, x = me // 4, (me // 2) % 2, me % 2
    more, less = z + 1 < chain, z > 0
    coords = ((x, y, 1, 2), (y, x, 2, 1), (y, x, 2, 1), (x, y, 1, 2))
    early, late = (0, 1), (2, 3)
    every = early + late

    def slot(p, zz, aa, bb):
        return zz * 4 + aa * coords[p][2] + bb * coords[p][3]

    def span(j):
        return pl.ds(pl.multiple_of(j * take, take), take)

    scols = [pl.ds(p * piece, piece) for p in every]
    gcols = scols[:-1] + [pl.ds(width - piece, full - width + piece)]

    barrier = pltpu.get_barrier_semaphore()
    pl.semaphore_signal(barrier, inc=1, device_id={"dp": 1 - dp}, device_id_type=MESH)
    for p in late:
        a, b = coords[p][0], coords[p][1]
        pl.semaphore_signal(
            barrier, inc=1, device_id={"expert": slot(p, z, a, 1 - b)}, device_id_type=MESH
        )

    @pl.when(more)
    def _():
        pl.semaphore_signal(barrier, inc=1, device_id={"expert": me + 4}, device_id_type=MESH)

    @pl.when(less)
    def _():
        pl.semaphore_signal(barrier, inc=1, device_id={"expert": me - 4}, device_id_type=MESH)

    pl.semaphore_wait(barrier, 3 + jnp.where(more, 1, 0) + jnp.where(less, 1, 0))

    pending = []
    used = {"g": 0, "s": 0}

    def send(kind, src, dst, recv, target, cond=None):
        sems = gsend if kind == "g" else ssend
        n = used[kind]
        used[kind] = n + 1

        def copy():
            return pltpu.make_async_remote_copy(
                src_ref=src, dst_ref=dst, send_sem=sems.at[n], recv_sem=recv,
                device_id=target, device_id_type=MESH,
            )

        def go():
            copy().start()

        def end():
            copy().wait_send()

        if cond is None:
            go()
        else:
            pl.when(cond)(go)
        pending.append((cond, end))

    def arrived(dst, recv):
        pltpu.make_async_remote_copy(
            src_ref=dst, dst_ref=dst, send_sem=wsem.at[0], recv_sem=recv,
            device_id={"dp": 1 - dp}, device_id_type=MESH,
        ).wait_recv()

    columns = pl.ds(pl.multiple_of(dp * mine, 128), mine)
    lines = pl.ds(pl.multiple_of(dp * mine, 128), mine)
    others = pl.ds(pl.multiple_of((1 - dp) * mine, 128), mine)
    pairs = (
        (gate_ref, wg.at[:, columns], wg.at[:, others]),
        (up_ref, wu.at[:, columns], wu.at[:, others]),
        (down_ref, wd.at[lines, :], wd.at[others, :]),
    )

    def local(i):
        return pltpu.make_async_copy(pairs[i][0], pairs[i][1], wsem.at[1 + i])

    def remote(i):
        return pltpu.make_async_remote_copy(
            src_ref=pairs[i][0], dst_ref=pairs[i][1], send_sem=wsem.at[4 + i],
            recv_sem=wsem.at[7 + i], device_id={"dp": 1 - dp}, device_id_type=MESH,
        )

    def start_weights():
        for i in range(3):
            remote(i).start()
            local(i).start()

    def wait_weights(i):
        local(i).wait()
        arrived(pairs[i][2], wsem.at[7 + i])
        remote(i).wait_send()

    def gather_send(c, p, src, j, target, cond=None):
        send("g", src, tok.at[c, span(j), gcols[p]], grecv.at[c, p, j], {"expert": target}, cond)

    def gather_start(c, p):
        a, b = coords[p][0], coords[p][1]
        src = x_ref.at[pl.ds(c * take, take), gcols[p]]
        gather_send(c, p, src, me, slot(p, z, 1 - a, b))
        gather_send(c, p, src, me, me + 4, more)
        gather_send(c, p, src, me, me - 4, less)
        gather_send(c, p, src, me, slot(p, z, a, 1 - b))

    def gather_wait(c, p, j):
        arrived(tok.at[c, span(j), gcols[p]], grecv.at[c, p, j])

    def gather_turn(c, p):
        a, b = coords[p][0], coords[p][1]
        j = slot(p, z, 1 - a, b)
        gather_wait(c, p, j)
        src = tok.at[c, span(j), gcols[p]]
        gather_send(c, p, src, j, me + 4, more)
        gather_send(c, p, src, j, me - 4, less)
        gather_send(c, p, src, j, slot(p, z, a, 1 - b))

    def gather_side(c, p, zz, aa, onward, target, cond):
        a, b = coords[p][0], coords[p][1]
        j = slot(p, zz, aa, b)
        pl.when(cond)(lambda: gather_wait(c, p, j))
        src = tok.at[c, span(j), gcols[p]]
        if p in late:
            gather_send(c, p, src, j, slot(p, z, 1 - a, b), cond)
        gather_send(c, p, src, j, target, jnp.logical_and(cond, onward))
        gather_send(c, p, src, j, slot(p, z, a, 1 - b), cond)

    def gather_chain(c, p, s):
        a = coords[p][0]
        for aa in (a, 1 - a) if p in early else (a,):
            gather_side(c, p, z - s, aa, more, me + 4, z - s >= 0)
            gather_side(c, p, z + s, aa, less, me - 4, z + s < chain)

    def gather_second(c, p, s):
        a, b = coords[p][0], coords[p][1]
        sides = ((z, None),) if s == 0 else ((z - s, z - s >= 0), (z + s, z + s < chain))
        for zz, cond in sides:
            j = slot(p, zz, 1 - a, b)
            if cond is None:
                gather_wait(c, p, j)
            else:
                pl.when(cond)(functools.partial(gather_wait, c, p, j))
            src = tok.at[c, span(j), gcols[p]]
            gather_send(c, p, src, j, slot(p, z, a, 1 - b), cond)

    def gather_last(c, p):
        a, b = coords[p][0], coords[p][1]
        for zz in range(chain):
            for aa in range(2):
                gather_wait(c, p, slot(p, zz, aa, 1 - b))

    def over(parts, f, *rest):
        return lambda: [f(rest[0], p, *rest[1:]) for p in parts]

    def gather_events(c):
        def own():
            tok[c, span(me), :] = x_ref[pl.ds(c * take, take), :]

        events = [lambda: (over(every, gather_start, c)(), own())]
        events.append(over(early, gather_turn, c))
        for s in range(1, chain):
            events.append(over(late, gather_chain, c, s))
            events.append(over(late, gather_second, c, s - 1))
            events.append(over(early, gather_chain, c, s))
        events.append(over(late, gather_second, c, chain - 1))
        events.append(over(every, gather_last, c))
        return events

    def shares(c):
        extra = tok[c, :, pl.ds(width, full - width)].astype(jnp.float32)
        lane = lax.broadcasted_iota(jnp.int32, extra.shape, 1)
        keep = jnp.logical_or(lane == me, lane == experts + me)
        return jnp.sum(jnp.where(keep, extra, 0.0), axis=1, keepdims=True)

    def expert_in(c, n):
        cut = pl.ds(n * htile, htile)
        values = tok[c, :, pl.ds(0, width)]
        gate = jnp.dot(values, wg[:, cut], preferred_element_type=jnp.float32)
        up = jnp.dot(values, wu[:, cut], preferred_element_type=jnp.float32)
        act = gate / (1.0 + jnp.exp(-gate)) * up * shares(c)
        hid[:, cut] = act.astype(hid.dtype)

    def expert_out(c, p):
        @pl.loop(0, piece // wtile)
        def _(n):
            cut = pl.ds(pl.multiple_of(p * piece + n * wtile, wtile), wtile)
            done = jnp.dot(hid[...], wd[:, cut], preferred_element_type=jnp.float32)
            part[c, :, cut] = done.astype(part.dtype)

    def expert_events(c):
        events = []
        for n in range(hidden // htile):
            events.append(functools.partial(expert_in, c, n))
        for p in every:
            events.append(lambda p=p: (expert_out(c, p), scatter_first(c, p)))
        return events

    def scatter_first(c, p):
        a, b = coords[p][0], coords[p][1]
        far = [(z + chain - 1 - i) % chain for i in range(chain)]
        dests = [(zz, aa) for aa in (1 - a, a) for zz in far]
        if p in early:
            dests = [(zz, aa) for zz in far for aa in (1 - a, a)]
        for zz, aa in dests:
            src = part.at[c, span(slot(p, zz, aa, 1 - b)), scols[p]]
            k = zz * 2 + aa
            send("s", src, rb.at[c, p, k], srecv.at[c, p, k],
                 {"expert": slot(p, z, a, 1 - b)})

    def scatter_second(c, p, i):
        a, b = coords[p][0], coords[p][1]
        zz = (z + chain - 1 - i) % chain
        k = zz * 2 + 1 - a
        arrived(rb.at[c, p, k], srecv.at[c, p, k])
        here = (c, span(slot(p, zz, 1 - a, b)), scols[p])
        both = part[here].astype(jnp.float32) + rb[c, p, k].astype(jnp.float32)
        part[here] = both.astype(part.dtype)
        send("s", part.at[here], ra.at[c, p, zz], srecv.at[c, p, 2 * chain + zz],
             {"expert": slot(p, z, 1 - a, b)})

    def summed(c, p, zz, aa):
        b = coords[p][1]
        k = zz * 2 + aa
        arrived(rb.at[c, p, k], srecv.at[c, p, k])
        own = part[c, span(slot(p, zz, aa, b)), scols[p]].astype(jnp.float32)
        total = own + rb[c, p, k].astype(jnp.float32)
        if p in late:
            arrived(ra.at[c, p, zz], srecv.at[c, p, 2 * chain + zz])
            total += ra[c, p, zz].astype(jnp.float32)
        return total

    def passing(c, p, way, zz, aa):
        k = (zz * 2 + aa) * 2 + way
        arrived(rz.at[c, p, k], srecv.at[c, p, 3 * chain + k])
        return rz[c, p, k].astype(jnp.float32)

    def scatter_side(c, p, way, zz, aa, cond, behind, target):
        here = (c, span(slot(p, zz, aa, coords[p][1])), scols[p])
        k = (zz * 2 + aa) * 2 + way

        @pl.when(jnp.logical_and(cond, jnp.logical_not(behind)))
        def _():
            part[here] = summed(c, p, zz, aa).astype(part.dtype)

        @pl.when(jnp.logical_and(cond, behind))
        def _():
            total = summed(c, p, zz, aa) + passing(c, p, way, zz, aa)
            part[here] = total.astype(part.dtype)

        send("s", part.at[here], rz.at[c, p, k], srecv.at[c, p, 3 * chain + k],
             {"expert": target}, cond)

    def scatter_chain(c, p, s):
        a = coords[p][0]
        for aa in (1 - a, a) if p in early else (a,):
            scatter_side(c, p, 0, z + s, aa, z + s < chain, less, me + 4)
            scatter_side(c, p, 1, z - s, aa, z - s >= 0, more, me - 4)

    def landed(c, p, aa):
        fin[:, :] = summed(c, p, z, aa)

        @pl.when(less)
        def _():
            fin[:, :] += passing(c, p, 0, z, aa)

        @pl.when(more)
        def _():
            fin[:, :] += passing(c, p, 1, z, aa)

    def scatter_turn(c, p):
        a, b = coords[p][0], coords[p][1]
        landed(c, p, 1 - a)
        here = (c, span(slot(p, z, 1 - a, b)), scols[p])
        part[here] = fin[:, :].astype(part.dtype)
        send("s", part.at[here], ra.at[c, p, 0], srecv.at[c, p, 2 * chain],
             {"expert": slot(p, z, 1 - a, b)})

    def scatter_last(c, p):
        lines = pl.ds(c * take, take)
        landed(c, p, coords[p][0])
        stream = res_ref[lines, scols[p]].astype(jnp.float32) + att_ref[
            lines, scols[p]
        ].astype(jnp.float32)
        total = stream + fin[:, :]
        if p in early:
            arrived(ra.at[c, p, 0], srecv.at[c, p, 2 * chain])
            total += ra[c, p, 0].astype(jnp.float32)
        o_ref[lines, scols[p]] = total.astype(o_ref.dtype)

    def scatter_events(c):
        events = []
        for s in range(chain - 1, 0, -1):
            events.append(over(early, scatter_chain, c, s))
            events.append(over(late, scatter_second, c, chain - 1 - s))
        events.append(over(late, scatter_second, c, chain - 1))
        events.append(over(early, scatter_turn, c))
        for s in range(chain - 1, 0, -1):
            events.append(over(late, scatter_chain, c, s))
        events.append(over(late, scatter_last, c))
        events.append(over(early, scatter_last, c))
        return events

    def merged(first, second):
        out = []
        for i in range(max(len(first), len(second))):
            out += first[i : i + 1] + second[i : i + 1]
        return out

    fetch = [gather_events(c) for c in range(CHUNKS)]
    work = [expert_events(c) for c in range(CHUNKS)]
    back = [scatter_events(c) for c in range(CHUNKS)]
    order = fetch[0][:1] + [start_weights] + fetch[0][1:3] + fetch[1][:1] + fetch[0][3:]
    order += [lambda: [wait_weights(i) for i in range(3)]]
    order += merged(fetch[1][1:], work[0])
    ahead = back[0][0:6:2] + back[0][1:6:2] + back[0][6:7]
    order += merged(work[1], ahead) + merged(back[0][7:], back[1][:7]) + back[1][7:]
    for event in order:
        event()
    for cond, end in pending:
        if cond is None:
            end()
        else:
            pl.when(cond)(end)


def multicast_shards(residual, attn_out, norm_gain, routes, mixing, gate_w, up_w, down_w):
    experts = lax.axis_size("expert")
    rows, width = residual.shape
    mine = gate_w.shape[2]
    hidden = mine * lax.axis_size("dp")
    lanes = -(-2 * experts // 128) * 128
    full = width + lanes
    take, chain = rows // CHUNKS, experts // 4
    _, normed = normalise(residual, attn_out, norm_gain)
    hit = routes[:, :, None] == jnp.arange(experts, dtype=jnp.int32)[None, None, :]
    share = jnp.sum(jnp.where(hit, mixing[:, :, None], 0.0), axis=1)
    high = lax.reduce_precision(share, 8, 7)
    extra = jnp.concatenate([high, share - high], axis=1).astype(jnp.bfloat16)
    extra = jnp.pad(extra, ((0, 0), (0, lanes - 2 * experts)))
    packed = jnp.concatenate([normed, extra], axis=1)
    bf16 = jnp.bfloat16
    copies = PARTS * CHUNKS * (7 + 8 * (chain - 1))
    sums = PARTS * CHUNKS * (1 + 3 * chain + 4 * (chain - 1))
    vmem, anywhere = pl.BlockSpec(memory_space=pltpu.VMEM), pl.BlockSpec(memory_space=pl.ANY)
    return pl.pallas_call(
        functools.partial(fused_kernel, experts),
        out_shape=jax.ShapeDtypeStruct((rows, width), bf16),
        in_specs=[vmem] * 3 + [anywhere] * 3,
        out_specs=vmem,
        scratch_shapes=[
            pltpu.VMEM((CHUNKS, experts * take, full), bf16),
            pltpu.VMEM((CHUNKS, experts * take, width), bf16),
            pltpu.VMEM((width, hidden), bf16),
            pltpu.VMEM((width, hidden), bf16),
            pltpu.VMEM((hidden, width), bf16),
            pltpu.VMEM((experts * take, hidden), bf16),
            pltpu.VMEM((CHUNKS, PARTS, 2 * chain, take, width // PARTS), bf16),
            pltpu.VMEM((CHUNKS, PARTS, chain, take, width // PARTS), bf16),
            pltpu.VMEM((CHUNKS, PARTS, 4 * chain, take, width // PARTS), bf16),
            pltpu.VMEM((take, width // PARTS), jnp.float32),
            pltpu.SemaphoreType.DMA((10,)),
            pltpu.SemaphoreType.DMA((copies,)),
            pltpu.SemaphoreType.DMA((CHUNKS, PARTS, experts)),
            pltpu.SemaphoreType.DMA((sums,)),
            pltpu.SemaphoreType.DMA((CHUNKS, PARTS, 7 * chain)),
        ],
        compiler_params=pltpu.CompilerParams(
            collective_id=0, has_side_effects=True, vmem_limit_bytes=66 * 1000 * 1000
        ),
    )(packed, residual, attn_out, gate_w[0], up_w[0], down_w[0])


def shards(residual, attn_out, norm_gain, routes, *rest):
    experts = lax.axis_size("expert")
    paired = lax.axis_size("dp") == 2 and experts % 4 == 0 and residual.shape[0] % 32 == 0
    wide = 2 * routes.shape[1] >= experts
    plan = multicast_shards if paired and wide else sparse_shards
    return plan(residual, attn_out, norm_gain, routes, *rest)


def solution(mesh):
    return jax.shard_map(
        shards,
        mesh=mesh,
        in_specs=(
            P(("dp", "expert"), None),
            P(("dp", "expert"), None),
            P(),
            P(("dp", "expert"), None),
            P(("dp", "expert"), None),
            P("expert", None, "dp"),
            P("expert", None, "dp"),
            P("expert", "dp", None),
        ),
        out_specs=P(("dp", "expert"), None),
        check_vma=False,
    )
```
